32 devices in a mesh: chan: 4 (over z), tblk: 8 (over y, x, core).
Axes of the slice: x: 2, y: 2, z: 4, core: 2. Of those that a mesh axis runs over, the one named last changes fastest.
Arguments:
- sky_image: float32 [4, 512, 1024], P(None, 'tblk', 'chan'), may hold values from 0 to 2
- dual_coefs: float32 [9, 4, 512, 1024], P(None, None, 'tblk', 'chan'), may hold values from -3 to 3
- phase_screen: float32 [4, 8, 512, 1024], P('chan', 'tblk'), may hold values from -3.140625 to 3.140625
- grid_rows: int32 [4, 8, 64], P('chan', 'tblk'), may hold values from 0 to 511
- grid_weight: float32 [4, 8, 1024, 256], P('chan', 'tblk'), may hold values from -0.1875 to 0.1875
- visibilities: float32 [4, 8, 2, 64, 256], P('chan', 'tblk'), may hold values from -6 to 6
- filters: float32 [9, 2, 3], replicated, may hold values from -1 to 1
- level_counts: int32 [9], replicated, may hold values from 1 to 3, as said below
- radius: float32 [9], replicated, may hold values from 0.5 to 4
Outputs:
- sky_update: float32 [4, 512, 1024], P(None, 'tblk', 'chan')
- dual_update: float32 [9, 4, 512, 1024], P(None, None, 'tblk', 'chan')
The draws below stay inside these ranges and needn't reach their ends.
Inputs may be any that keep to these rules, and one draw needn't show every extreme that they name: `level_counts`: at least one basis has 3 levels.
All inputs are finite; a program needn't handle non-finite values.
Results may differ from the reference program's by a relative error of at most 0.00011.
Values sent between devices are 32-bit elements; how exact they have to be, the bound alone decides.
A program may use at most 128 MiB of HBM per device.

```python
import math
import jax
import jax.numpy as jnp
from jax import lax

NX = 512
NY = 1024
RVIS = 64
VIS = 256
NBASIS = 9
LEVELS = 3
ITERS = 2
HALO = 4
CH = 4
NBLK = 8


def draw_level_counts(key, part):
    first_key = jax.random.fold_in(key, 11)
    second_key = jax.random.fold_in(key, 23)
    drawn = jax.random.randint(first_key, (NBASIS,), 1, LEVELS + 1)
    chosen = jax.random.randint(second_key, (), 0, NBASIS)
    return jnp.where(jnp.arange(NBASIS) == chosen, LEVELS, drawn).astype(jnp.int32)


def place_ends(values, own_key, least, top_value):
    shape = values.shape
    place = [jax.random.randint(jax.random.fold_in(own_key, axis), (), 0, shape[axis]) for axis in range(len(shape))]
    values = values.at[tuple(place)].set(least)
    longest = shape.index(max(shape))
    place[longest] = (place[longest] + 1) % shape[longest]
    return values.at[tuple(place)].set(top_value)


def shard_levels(rng, extent, shards, smallest, top_value):
    def one(dim, shards_of):
        heights = jax.random.uniform(jax.random.fold_in(jax.random.fold_in(rng, 6), dim), (shards_of,), jnp.float32, smallest / len(shards), top_value / len(shards))
        return jnp.repeat(jnp.exp(heights), extent[dim] // shards_of).reshape((-1,) + (1,) * (len(extent) - dim - 1))

    factor_of = one(*shards[0])
    for cut in shards[1:]:
        factor_of = factor_of * one(*cut)
    return factor_of


def centred(own_key, shape, scale, reach, split=(), kind=jnp.bfloat16):
    values = scale * jax.random.normal(own_key, shape, jnp.float32)
    if split:
        values = values * shard_levels(own_key, shape, split, -0.22, 0.18)
    return jnp.clip(values, -reach, reach).astype(kind)


def setup_inputs(seed: int = 0) -> dict:
    streams_of = jax.random.split(jax.random.key(seed), 10)
    return {
        "sky_image": jnp.clip(2.0 * jax.random.uniform(streams_of[0], (CH, NX, NY), jnp.float32) ** shard_levels(streams_of[0], (CH, NX, NY), ((1, 8), (2, 4)), -0.2, 0.2), 0.0, 2.0),
        "dual_coefs": centred(streams_of[1], (NBASIS, CH, NX, NY), 0.5, 3.0, ((2, 8), (3, 4)), jnp.float32),
        "phase_screen": jnp.clip(jax.random.uniform(streams_of[2], (CH, NBLK, NX, NY), jnp.float32, -3.140625, 3.140625), -3.140625, 3.140625),
        "grid_rows": place_ends(jax.random.randint(streams_of[3], (CH, NBLK, RVIS), 0, NX), jax.random.fold_in(streams_of[3], 1), 0, NX - 1).astype(jnp.int32),
        "grid_weight": centred(streams_of[4], (CH, NBLK, NY, VIS), NY ** -0.5, 0.1875, ((0, 4), (1, 8)), jnp.float32),
        "visibilities": centred(streams_of[5], (CH, NBLK, 2, RVIS, VIS), 1.0, 6.0, ((0, 4), (1, 8)), jnp.float32),
        "filters": jnp.clip(jax.random.uniform(streams_of[6], (NBASIS, 2, 3), jnp.float32, -1.0, 1.0), -1.0, 1.0),
        "level_counts": draw_level_counts(jax.random.fold_in(streams_of[9], 71), 0),
        "radius": jnp.clip(jnp.exp(jax.random.uniform(streams_of[8], (NBASIS,), jnp.float32, math.log(0.5), math.log(4.0))), 0.5, 4.0),
    }


FULL_PRECISION = lax.Precision.HIGHEST
STEP_PRIMAL = 0.5
STEP_DUAL = 0.5

def filter_forward(padded, filter_taps, stride, rows_out, cols_out):
    across = jnp.zeros(padded.shape[:2] + (cols_out,), jnp.float32)
    for offset in (-1, 0, 1):
        first_col = (HALO + offset * stride).astype(jnp.int32)
        across = across + filter_taps[1, offset + 1] * lax.dynamic_slice_in_dim(padded, first_col, cols_out, 2)
    result = jnp.zeros((padded.shape[0], rows_out, cols_out), jnp.float32)
    for offset in (-1, 0, 1):
        first_row = (HALO + offset * stride).astype(jnp.int32)
        result = result + filter_taps[0, offset + 1] * lax.dynamic_slice_in_dim(across, first_row, rows_out, 1)
    return result

def filter_back(padded, filter_taps, stride, rows_out, cols_out):
    across = jnp.zeros(padded.shape[:2] + (cols_out,), jnp.float32)
    for offset in (-1, 0, 1):
        first_col = (HALO - offset * stride).astype(jnp.int32)
        across = across + filter_taps[1, offset + 1] * lax.dynamic_slice_in_dim(padded, first_col, cols_out, 2)
    result = jnp.zeros((padded.shape[0], rows_out, cols_out), jnp.float32)
    for offset in (-1, 0, 1):
        first_row = (HALO - offset * stride).astype(jnp.int32)
        result = result + filter_taps[0, offset + 1] * lax.dynamic_slice_in_dim(across, first_row, rows_out, 1)
    return result

def block_gradient(image_chan, phase_block, rows_block, weight_block, data_block):
    cos_screen = jnp.cos(phase_block)
    sin_screen = jnp.sin(phase_block)
    screened = lax.complex(cos_screen * image_chan, sin_screen * image_chan)
    spectrum = jnp.fft.fft2(screened, norm='ortho')
    picked = spectrum[rows_block]
    misfit_real = jnp.dot(jnp.real(picked), weight_block, precision=FULL_PRECISION) - data_block[0]
    misfit_imag = jnp.dot(jnp.imag(picked), weight_block, precision=FULL_PRECISION) - data_block[1]
    gridded_real = jnp.dot(misfit_real, weight_block.T, precision=FULL_PRECISION)
    gridded_imag = jnp.dot(misfit_imag, weight_block.T, precision=FULL_PRECISION)
    grid_full = jnp.zeros(spectrum.shape, spectrum.dtype).at[rows_block].add(lax.complex(gridded_real, gridded_imag))
    pulled = jnp.fft.ifft2(grid_full, norm='ortho')
    return cos_screen * jnp.real(pulled) + sin_screen * jnp.imag(pulled)

def channel_gradient(pieces):
    image_chan, phase_chan, rows_chan, weight_chan, data_chan = pieces

    def add_block(totals, block_pieces):
        phase_block, rows_block, weight_block, data_block = block_pieces
        return (totals + block_gradient(image_chan, phase_block, rows_block, weight_block, data_block), None)
    totals, unused = lax.scan(add_block, jnp.zeros_like(image_chan), (phase_chan, rows_chan, weight_chan, data_chan))
    return totals

def analyse(field, filters, spacing):
    padded = jnp.pad(field, ((0, 0), (HALO, HALO), (HALO, HALO)))
    return jnp.stack([filter_forward(padded, filters[basis_index], spacing[basis_index], field.shape[1], field.shape[2]) for basis_index in range(NBASIS)])

def synthesise(coefs, filters, spacing):
    padded = jnp.pad(coefs, ((0, 0), (0, 0), (HALO, HALO), (HALO, HALO)))
    totals = jnp.zeros(coefs.shape[1:], jnp.float32)
    for basis_index in range(NBASIS):
        totals = totals + filter_back(padded[basis_index], filters[basis_index], spacing[basis_index], coefs.shape[2], coefs.shape[3])
    return totals

def reference(sky_image, dual_coefs, phase_screen, grid_rows, grid_weight, visibilities, filters, level_counts, radius):
    spacing = lax.shift_left(jnp.ones_like(level_counts), level_counts - 1)
    radius_cells = radius[:, None, None, None]
    current = sky_image
    dual_now = dual_coefs
    for sweep_index in range(ITERS):
        gradient = lax.map(channel_gradient, (current, phase_screen, grid_rows, grid_weight, visibilities))
        synthesised = synthesise(dual_now, filters, spacing)
        updated = jnp.maximum(current - STEP_PRIMAL * (gradient + synthesised), 0.0)
        leading = 2.0 * updated - current
        raised = dual_now + STEP_DUAL * analyse(leading, filters, spacing)
        norm_cells = jnp.sqrt(lax.optimization_barrier(jnp.sum(raised * raised, axis=1, keepdims=True)))
        dual_now = raised * radius_cells / jnp.maximum(norm_cells, radius_cells)
        current = updated
    return (current, dual_now)
```

```python
import functools
import math

import jax
import jax.numpy as jnp
from jax import lax
from jax.experimental import pallas as pl
from jax.experimental.pallas import tpu as pltpu
from jax.sharding import PartitionSpec as P

ITERS = 2
HALO = 4
EDGE = 8
LANES = 128
LEVELS = 3
STEP_PRIMAL = 0.5
STEP_DUAL = 0.5
F32 = jnp.float32
BF16 = jnp.bfloat16
VMEM = pl.BlockSpec(memory_space=pltpu.VMEM)
SMEM = pl.BlockSpec(memory_space=pltpu.SMEM)


def sincos(angle):
    turn = jnp.floor(angle * (2.0 / math.pi) + 0.5)
    rest = angle - turn * 1.5703125
    rest = rest - turn * 4.83751296997e-04
    rest = rest - turn * 7.54978995489e-08
    square = rest * rest
    sine = rest + rest * square * (
        -1.6666654611e-1 + square * (8.3321608736e-3 - square * 1.9515295891e-4)
    )
    cosine = (1.0 - 0.5 * square) + square * square * (
        4.166664568298827e-2 + square * (-1.388731625493765e-3 + square * 2.443315711809948e-5)
    )
    odd = jnp.abs(turn) == 1.0
    far = jnp.abs(turn) == 2.0
    sin_out = jnp.where(odd, turn * cosine, jnp.where(far, -sine, sine))
    cos_out = jnp.where(odd, -turn * sine, jnp.where(far, -cosine, cosine))
    return sin_out, cos_out


def root_of_unity(number, count):
    number = lax.rem(number, jnp.int32(count))
    number = jnp.where(number >= count // 2, number - count, number)
    return sincos(number.astype(F32) * (2.0 * math.pi / count))


def halves(value):
    high = value.astype(BF16)
    return high, (value - high.astype(F32)).astype(BF16)


def dot(left, right, transposed=False):
    dims = (((1,), (1 if transposed else 0,)), ((), ()))
    return lax.dot_general(left, right, dims, preferred_element_type=F32)


def dot_three(left, right_high, right_low, transposed=False):
    rows = left.shape[0]
    high, low = halves(left)
    both = dot(jnp.concatenate([high, low], axis=0), right_high, transposed)
    return both[:rows] + both[rows:] + dot(high, right_low, transposed)


def prepare_body(phase, weight, rows_col, rows_lane, cos_ref, sin_ref, g_high, g_low, r_ref, rt_ref, slabs):
    full_rows, full_cols = phase.shape
    vis = weight.shape[1]
    picked = rows_col.shape[0]
    step = 16

    def screen(i, carry):
        at = pl.ds(pl.multiple_of(i * step, step), step)
        sine, cosine = sincos(phase[at, :])
        cos_ref[at, :] = cosine
        sin_ref[at, :] = sine
        return carry

    lax.fori_loop(0, full_rows // step, screen, 0)

    sine, cosine = root_of_unity(
        rows_col[:, 0:1] * lax.broadcasted_iota(jnp.int32, (picked, full_rows), 1), full_rows
    )
    scale = 1.0 / math.sqrt(full_rows)
    high, low = halves(jnp.concatenate([cosine * scale, -sine * scale], axis=0))
    r_ref[...] = jnp.concatenate([high, low], axis=0)
    sine, cosine = root_of_unity(
        rows_lane[0:1, :] * lax.broadcasted_iota(jnp.int32, (full_rows, picked), 0), full_rows
    )
    high, low = halves(jnp.concatenate([cosine * scale, -sine * scale], axis=1))
    rt_ref[...] = jnp.concatenate([high, high, low], axis=1)

    half = full_cols // 2
    scale = 1.0 / math.sqrt(full_cols)
    count = vis // LANES
    for k in range(count):
        slabs[k] = weight[:, k * LANES : (k + 1) * LANES] * scale
    even_high, even_low = halves(
        jnp.concatenate([slabs[k, pl.ds(0, half, 2), :] for k in range(count)], axis=1)
    )
    odd_high, odd_low = halves(
        jnp.concatenate([slabs[k, pl.ds(1, half, 2), :] for k in range(count)], axis=1)
    )
    tile = 64

    def transform(i, carry):
        base = pl.multiple_of(i * tile, tile)
        line = base + lax.broadcasted_iota(jnp.int32, (tile, half), 0)
        cell = 2 * lax.broadcasted_iota(jnp.int32, (tile, half), 1)
        sine, cosine = root_of_unity(line * cell, full_cols)
        even = dot_three(jnp.concatenate([cosine, -sine], axis=0), even_high, even_low)
        sine, cosine = root_of_unity(line * (cell + 1), full_cols)
        odd = dot_three(jnp.concatenate([cosine, -sine], axis=0), odd_high, odd_low)
        for where, total in ((base, even + odd), (base + half, even - odd)):
            where = pl.multiple_of(where, tile)
            high, low = halves(jnp.concatenate([total[:tile], total[tile:]], axis=1))
            g_high[pl.ds(where, tile), :] = high
            g_low[pl.ds(where, tile), :] = low
        return carry

    lax.fori_loop(0, half // tile, transform, 0)


def forward_body(image, cos_ref, sin_ref, g_high, g_low, r_ref, data, total):
    full_rows, full_cols = cos_ref.shape
    picked = r_ref.shape[0] // 4
    vis = g_high.shape[1] // 2
    chunk = 256
    total[...] = jnp.zeros_like(total)
    stacked = r_ref[...]
    high_rows = r_ref[0 : 2 * picked, :]

    def add(i, carry):
        at = pl.ds(pl.multiple_of(i * chunk, chunk), chunk)
        block = image[:, at]

        def rows_of(screen):
            high, low = halves(block * screen[:, at])
            both = dot(stacked, high)
            return both[: 2 * picked] + both[2 * picked :] + dot(high_rows, low)

        real = rows_of(cos_ref)
        imag = rows_of(sin_ref)
        spectrum = jnp.concatenate(
            [real[:picked] - imag[picked:], imag[:picked] + real[picked:]], axis=0
        )
        total[...] += dot_three(spectrum, g_high[at, :], g_low[at, :])
        return carry

    lax.fori_loop(0, full_cols // chunk, add, 0)
    sums = total[...]
    real = sums[:picked, :vis] - sums[picked:, vis:] - data[0]
    imag = sums[:picked, vis:] + sums[picked:, :vis] - data[1]
    total[...] = jnp.concatenate(
        [jnp.concatenate([real, imag], axis=1), jnp.concatenate([imag, -real], axis=1)], axis=0
    )


def backward_chunk(misfit, at, cos_ref, sin_ref, g_high, g_low, rt_ref):
    picked = misfit.shape[0] // 2
    back = dot_three(misfit, g_high[at, :], g_low[at, :], True)
    swapped = jnp.concatenate([back[picked:], -back[:picked]], axis=0)
    high, low = halves(jnp.concatenate([back, swapped], axis=1))
    grid = dot(rt_ref[...], jnp.concatenate([high, low, high], axis=0))
    chunk = back.shape[1]
    return cos_ref[:, at] * grid[:, :chunk] + sin_ref[:, at] * grid[:, chunk:]


def measure_body(image, cos_ref, sin_ref, g_high, g_low, r_ref, rt_ref, data, out, total):
    forward_body(image, cos_ref, sin_ref, g_high, g_low, r_ref, data, total)
    chunk = 256

    def back(i, carry):
        at = pl.ds(pl.multiple_of(i * chunk, chunk), chunk)
        out[:, at] = backward_chunk(total[...], at, cos_ref, sin_ref, g_high, g_low, rt_ref)
        return carry

    lax.fori_loop(0, out.shape[1] // chunk, back, 0)


def lane_index(width):
    return lax.broadcasted_iota(jnp.int32, (1, width), 1)


def turned(value, distance):
    distance = distance % value.shape[-1]
    return value if distance == 0 else pltpu.roll(value, distance, value.ndim - 1)


def synthesis_body(dual, taps, levels, out, spill_right, spill_left, padded, plus, minus):
    bases, channels, rows, cols = dual.shape
    tall = rows + 2 * EDGE
    out[...] = jnp.zeros_like(out)
    plus[...] = jnp.zeros_like(plus)
    minus[...] = jnp.zeros_like(minus)
    padded[:, : 2 * EDGE, :] = jnp.zeros((channels, 2 * EDGE, cols), F32)
    padded[:, rows + 2 * EDGE :, :] = jnp.zeros((channels, 2 * EDGE, cols), F32)

    def one(q, carry):
        padded[:, 2 * EDGE : 2 * EDGE + rows, :] = dual[q]
        for level in range(LEVELS):

            @pl.when(levels[q] == level + 1)
            def _():
                gap = 2**level
                for c in range(channels):
                    mixed = taps[6 * q + 1] * padded[c, EDGE : EDGE + tall, :]
                    mixed += taps[6 * q] * padded[c, EDGE + gap : EDGE + gap + tall, :]
                    mixed += taps[6 * q + 2] * padded[c, EDGE - gap : EDGE - gap + tall, :]
                    out[c] += taps[6 * q + 4] * mixed
                    minus[level, c] += taps[6 * q + 3] * mixed
                    plus[level, c] += taps[6 * q + 5] * mixed

        return carry

    lax.fori_loop(0, bases, one, 0)
    lane = lane_index(cols)
    near = lane_index(LANES)
    right = jnp.zeros((tall, LANES), F32)
    left = jnp.zeros((tall, LANES), F32)
    for c in range(channels):
        total = out[c]
        to_right = jnp.zeros((tall, LANES), F32)
        to_left = jnp.zeros((tall, LANES), F32)
        for level in range(LEVELS):
            gap = 2**level
            moved = turned(plus[level, c], gap)
            total += jnp.where(lane >= gap, moved, 0.0)
            to_right += jnp.where(near < gap, moved[:, :LANES], 0.0)
            moved = turned(minus[level, c], -gap)
            total += jnp.where(lane < cols - gap, moved, 0.0)
            to_left += jnp.where(near >= LANES - gap, moved[:, cols - LANES :], 0.0)
        out[c] = total
        right += turned(to_right, HALO * c)
        left += turned(to_left, -HALO * c)
    spill_right[...] = right
    spill_left[...] = left


def widen(tile, cols, at_end):
    if cols == LANES:
        return tile
    rest = jnp.zeros((tile.shape[0], cols - LANES), F32)
    return jnp.concatenate([rest, tile] if at_end else [tile, rest], axis=1)


def update_body(
    now, gradient, synth, side_low, side_high, top, bottom, updated, leading, pack_left, pack_right
):
    channels, rows, cols = now.shape
    near = lane_index(LANES)
    to_left = jnp.zeros((rows, LANES), F32)
    to_right = jnp.zeros((rows, LANES), F32)
    none = jnp.zeros((rows - EDGE, cols), F32)

    def folded(side):
        inside = side[EDGE : EDGE + rows, :]
        rest = jnp.zeros((rows - EDGE, LANES), F32)
        inside += jnp.concatenate([side[:EDGE, :], rest], axis=0)
        inside += jnp.concatenate([rest, side[EDGE + rows :, :]], axis=0)
        return inside

    low = folded(side_low)
    high = folded(side_high)
    for c in range(channels):
        total = synth[c, EDGE : EDGE + rows, :]
        total += jnp.concatenate([top[c], none], axis=0)
        total += jnp.concatenate([none, bottom[c]], axis=0)
        total += widen(jnp.where(near < HALO, turned(low, -HALO * c), 0.0), cols, False)
        total += widen(jnp.where(near >= LANES - HALO, turned(high, HALO * c), 0.0), cols, True)
        before = now[c]
        after = jnp.maximum(before - STEP_PRIMAL * (gradient[c] + total), 0.0)
        updated[c] = after
        ahead = 2.0 * after - before
        leading[c] = ahead
        to_left += turned(jnp.where(near < HALO, ahead[:, :LANES], 0.0), HALO * c)
        to_right += turned(
            jnp.where(near >= LANES - HALO, ahead[:, cols - LANES :], 0.0), -HALO * c
        )
    pack_left[...] = to_left
    pack_right[...] = to_right


def analysis_body(
    leading, side_low, side_high, top, bottom, dual, taps, levels, radius, out, fields, mixed
):
    bases, channels, rows, cols = dual.shape
    near = lane_index(LANES)
    for c in range(channels):
        field = jnp.concatenate([top[c], leading[c], bottom[c]], axis=0)
        before = turned(side_low[...], HALO * c)
        behind = turned(side_high[...], -HALO * c)
        fields[0, c] = field
        for level in range(LEVELS):
            gap = 2**level
            moved = turned(field, gap)
            first = jnp.where(near < gap, turned(before, gap), moved[:, :LANES])
            if cols > LANES:
                first = jnp.concatenate([first, moved[:, LANES:]], axis=1)
            fields[1 + 2 * level, c] = first
            moved = turned(field, -gap)
            last = jnp.where(near >= LANES - gap, turned(behind, -gap), moved[:, cols - LANES :])
            if cols > LANES:
                last = jnp.concatenate([moved[:, : cols - LANES], last], axis=1)
            fields[2 + 2 * level, c] = last

    def one(q, carry):
        for level in range(LEVELS):

            @pl.when(levels[q] == level + 1)
            def _():
                gap = 2**level
                for c in range(channels):
                    mixed[c] = (
                        taps[6 * q + 3] * fields[1 + 2 * level, c]
                        + taps[6 * q + 4] * fields[0, c]
                        + taps[6 * q + 5] * fields[2 + 2 * level, c]
                    )
                for c in range(channels):
                    value = taps[6 * q] * mixed[c, EDGE - gap : EDGE - gap + rows, :]
                    value += taps[6 * q + 1] * mixed[c, EDGE : EDGE + rows, :]
                    value += taps[6 * q + 2] * mixed[c, EDGE + gap : EDGE + gap + rows, :]
                    out[q, c] = dual[q, c] + STEP_DUAL * value

        energy = out[q, 0] * out[q, 0]
        for c in range(1, channels):
            energy += out[q, c] * out[q, c]
        factor = radius[q] / jnp.maximum(jnp.sqrt(energy), radius[q])
        for c in range(channels):
            out[q, c] = out[q, c] * factor
        return carry

    lax.fori_loop(0, bases, one, 0)


def local_call(body, shapes, in_specs, scratch, name):
    return pl.pallas_call(
        body,
        out_shape=shapes,
        in_specs=in_specs,
        out_specs=jax.tree.map(lambda _: VMEM, shapes),
        scratch_shapes=scratch,
        compiler_params=pltpu.CompilerParams(vmem_limit_bytes=58 * 1024 * 1024),
        name=name,
    )


def arr(*shape, dtype=F32):
    return jax.ShapeDtypeStruct(shape, dtype)


def neighbour(value, across, along):
    nc, nt = lax.axis_size("chan"), lax.axis_size("tblk")
    route = [
        (c * nt + t, (c + across) * nt + t + along)
        for c in range(nc)
        for t in range(nt)
        if 0 <= c + across < nc and 0 <= t + along < nt
    ]
    return lax.ppermute(value, ("chan", "tblk"), route)


def sides(pack_a, pack_b, rows):
    low = jnp.concatenate(
        [
            neighbour(pack_a[2], 1, 1),
            neighbour(pack_a[1], 1, 0),
            neighbour(pack_a[0], 1, -1),
        ],
        axis=0,
    )
    high = jnp.concatenate(
        [
            neighbour(pack_b[2], -1, 1),
            neighbour(pack_b[1], -1, 0),
            neighbour(pack_b[0], -1, -1),
        ],
        axis=0,
    )
    return low, high


def per_device(sky, dual, phase, rows_at, weight, vis_data, filters, level_counts, radius):
    channels, rows, cols = sky.shape
    bases = dual.shape[0]
    full_rows, full_cols = phase.shape[2:]
    vis = weight.shape[3]
    picked = rows_at.shape[2]
    tall = rows + 2 * EDGE
    taps = filters.reshape(-1)
    data = vis_data[0, 0]
    image_shape = arr(full_rows, full_cols)
    cos_s, sin_s, g_high, g_low, r_mat, rt_mat = local_call(
        prepare_body,
        (
            image_shape,
            image_shape,
            arr(full_cols, 2 * vis, dtype=BF16),
            arr(full_cols, 2 * vis, dtype=BF16),
            arr(4 * picked, full_rows, dtype=BF16),
            arr(full_rows, 6 * picked, dtype=BF16),
        ),
        [VMEM] * 4,
        [pltpu.VMEM((vis // LANES, full_cols, LANES), F32)],
        "prepare",
    )(phase[0, 0], weight[0, 0], rows_at[0, 0][:, None], rows_at[0, 0][None, :])
    for _ in range(ITERS):
        spread = lax.all_to_all(sky, "chan", split_axis=0, concat_axis=2, tiled=True)
        whole = lax.all_gather(spread[0], "tblk", axis=0, tiled=True)
        synth, spill_right, spill_left = local_call(
            synthesis_body,
            (arr(channels, tall, cols), arr(tall, LANES), arr(tall, LANES)),
            [VMEM, SMEM, SMEM],
            [
                pltpu.VMEM((channels, rows + 4 * EDGE, cols), F32),
                pltpu.VMEM((LEVELS, channels, tall, cols), F32),
                pltpu.VMEM((LEVELS, channels, tall, cols), F32),
            ],
            "synthesis",
        )(dual, taps, level_counts)
        cut = lambda spill: (spill[:EDGE], spill[EDGE : EDGE + rows], spill[EDGE + rows :])
        low, high = sides(cut(spill_right), cut(spill_left), rows)
        low = jnp.concatenate([low[:EDGE], low[EDGE : EDGE + rows], low[EDGE + rows :]], axis=0)
        top = neighbour(synth[:, EDGE + rows :], 0, 1)
        bottom = neighbour(synth[:, :EDGE], 0, -1)
        part = local_call(
            measure_body,
            image_shape,
            [VMEM] * 8,
            [pltpu.VMEM((2 * picked, 2 * vis), F32)],
            "measure",
        )(whole, cos_s, sin_s, g_high, g_low, r_mat, rt_mat, data)
        summed = lax.psum_scatter(part, "tblk", scatter_dimension=0, tiled=True)
        gradient = lax.all_to_all(summed[None], "chan", split_axis=2, concat_axis=0, tiled=True)
        updated, leading, pack_left, pack_right = local_call(
            update_body,
            (sky_shape := arr(channels, rows, cols), sky_shape, arr(rows, LANES), arr(rows, LANES)),
            [VMEM] * 7,
            [],
            "update",
        )(sky, gradient, synth, low, high, top, bottom)
        edges = lambda pack: (pack[:EDGE], pack, pack[rows - EDGE :])
        low, high = sides(edges(pack_right), edges(pack_left), rows)
        top = neighbour(leading[:, rows - EDGE :], 0, 1)
        bottom = neighbour(leading[:, :EDGE], 0, -1)
        dual = local_call(
            analysis_body,
            arr(*dual.shape),
            [VMEM] * 6 + [SMEM] * 3,
            [
                pltpu.VMEM((1 + 2 * LEVELS, channels, tall, cols), F32),
                pltpu.VMEM((channels, tall, cols), F32),
            ],
            "analysis",
        )(leading, low, high, top, bottom, dual, taps, level_counts, radius)
        sky = updated
    return sky, dual


def solution(mesh):
    placed = (
        P(None, "tblk", "chan"),
        P(None, None, "tblk", "chan"),
        P("chan", "tblk", None, None),
        P("chan", "tblk", None),
        P("chan", "tblk", None, None),
        P("chan", "tblk", None, None, None),
        P(),
        P(),
        P(),
    )
    return jax.shard_map(
        per_device,
        mesh=mesh,
        in_specs=placed,
        out_specs=(P(None, "tblk", "chan"), P(None, None, "tblk", "chan")),
        check_vma=False,
    )
```

```python
import functools
import math

import jax
import jax.numpy as jnp
from jax import lax
from jax.experimental import pallas as pl
from jax.experimental.pallas import tpu as pltpu
from jax.sharding import PartitionSpec as P

ITERS = 2
HALO = 4
EDGE = 8
LANES = 128
LEVELS = 3
STEP_PRIMAL = 0.5
STEP_DUAL = 0.5
F32 = jnp.float32
BF16 = jnp.bfloat16
VMEM = pl.BlockSpec(memory_space=pltpu.VMEM)
SMEM = pl.BlockSpec(memory_space=pltpu.SMEM)


def sincos(angle):
    turn = jnp.floor(angle * (2.0 / math.pi) + 0.5)
    rest = angle - turn * 1.5703125
    rest = rest - turn * 4.83751296997e-04
    rest = rest - turn * 7.54978995489e-08
    square = rest * rest
    sine = rest + rest * square * (
        -1.6666654611e-1 + square * (8.3321608736e-3 - square * 1.9515295891e-4)
    )
    cosine = (1.0 - 0.5 * square) + square * square * (
        4.166664568298827e-2 + square * (-1.388731625493765e-3 + square * 2.443315711809948e-5)
    )
    odd = jnp.abs(turn) == 1.0
    far = jnp.abs(turn) == 2.0
    sin_out = jnp.where(odd, turn * cosine, jnp.where(far, -sine, sine))
    cos_out = jnp.where(odd, -turn * sine, jnp.where(far, -cosine, cosine))
    return sin_out, cos_out


def root_of_unity(number, count):
    number = lax.rem(number, jnp.int32(count))
    number = jnp.where(number >= count // 2, number - count, number)
    return sincos(number.astype(F32) * (2.0 * math.pi / count))


def halves(value):
    high = value.astype(BF16)
    return high, (value - high.astype(F32)).astype(BF16)


def dot(left, right, transposed=False):
    dims = (((1,), (1 if transposed else 0,)), ((), ()))
    return lax.dot_general(left, right, dims, preferred_element_type=F32)


def dot_three(left, right_high, right_low, transposed=False):
    rows = left.shape[0]
    high, low = halves(left)
    both = dot(jnp.concatenate([high, low], axis=0), right_high, transposed)
    return both[:rows] + both[rows:] + dot(high, right_low, transposed)


def screens(phase, cos_ref, sin_ref):
    step = 16

    def screen(i, carry):
        at = pl.ds(pl.multiple_of(i * step, step), step)
        sine, cosine = sincos(phase[at, :])
        cos_ref[at, :] = cosine
        sin_ref[at, :] = sine
        return carry

    lax.fori_loop(0, phase.shape[0] // step, screen, 0)


def transforms(weight, rows_col, rows_lane, g_high, g_low, r_ref, rt_ref, slabs):
    full_rows = rt_ref.shape[0]
    full_cols, vis = weight.shape
    picked = rows_col.shape[0]
    sine, cosine = root_of_unity(
        rows_col[:, 0:1] * lax.broadcasted_iota(jnp.int32, (picked, full_rows), 1), full_rows
    )
    scale = 1.0 / math.sqrt(full_rows)
    high, low = halves(jnp.concatenate([cosine * scale, -sine * scale], axis=0))
    r_ref[...] = jnp.concatenate([high, low], axis=0)
    sine, cosine = root_of_unity(
        rows_lane[0:1, :] * lax.broadcasted_iota(jnp.int32, (full_rows, picked), 0), full_rows
    )
    high, low = halves(jnp.concatenate([cosine * scale, -sine * scale], axis=1))
    rt_ref[...] = jnp.concatenate([high, high, low], axis=1)

    half = full_cols // 2
    scale = 1.0 / math.sqrt(full_cols)
    count = vis // LANES
    for k in range(count):
        slabs[k] = weight[:, k * LANES : (k + 1) * LANES] * scale
    even_high, even_low = halves(
        jnp.concatenate([slabs[k, pl.ds(0, half, 2), :] for k in range(count)], axis=1)
    )
    odd_high, odd_low = halves(
        jnp.concatenate([slabs[k, pl.ds(1, half, 2), :] for k in range(count)], axis=1)
    )
    tile = 64

    def transform(i, carry):
        base = pl.multiple_of(i * tile, tile)
        line = base + lax.broadcasted_iota(jnp.int32, (tile, half), 0)
        cell = 2 * lax.broadcasted_iota(jnp.int32, (tile, half), 1)
        sine, cosine = root_of_unity(line * cell, full_cols)
        even = dot_three(jnp.concatenate([cosine, -sine], axis=0), even_high, even_low)
        sine, cosine = root_of_unity(line * (cell + 1), full_cols)
        odd = dot_three(jnp.concatenate([cosine, -sine], axis=0), odd_high, odd_low)
        for where, total in ((base, even + odd), (base + half, even - odd)):
            where = pl.multiple_of(where, tile)
            high, low = halves(jnp.concatenate([total[:tile], total[tile:]], axis=1))
            g_high[pl.ds(where, tile), :] = high
            g_low[pl.ds(where, tile), :] = low
        return carry

    lax.fori_loop(0, half // tile, transform, 0)


def lane_index(width):
    return lax.broadcasted_iota(jnp.int32, (1, width), 1)


def turned(value, distance):
    distance = distance % value.shape[-1]
    return value if distance == 0 else pltpu.roll(value, distance, value.ndim - 1)


def gap_of(level):
    return level + jnp.where(level == LEVELS, 1, 0)


def synthesis_body(dual, taps, levels, out, spill_right, spill_left, padded, plus, minus):
    bases, channels, rows, cols = dual.shape
    tall = rows + 2 * EDGE
    step = 16
    zeros = jnp.zeros((bases, channels, 2 * EDGE, cols), F32)
    padded[:, :, : 2 * EDGE, :] = zeros
    padded[:, :, rows + 2 * EDGE :, :] = zeros
    padded[:, :, 2 * EDGE : 2 * EDGE + rows, :] = dual[...]

    def one(i, carry):
        c = lax.rem(i, channels)
        row = pl.multiple_of(lax.div(i, channels) * step, step)
        none = jnp.zeros((step, cols), F32)
        centre, ahead, behind = none, [none] * LEVELS, [none] * LEVELS
        for q in range(bases):
            gap = gap_of(levels[q])
            block = padded[q, c, pl.ds(row, step + 2 * EDGE), :]
            value = taps[6 * q + 1] * block[EDGE : EDGE + step]
            lower = pltpu.roll(block, step + 2 * EDGE - gap, 0)
            value += taps[6 * q] * lower[EDGE : EDGE + step]
            upper = pltpu.roll(block, gap, 0)
            value += taps[6 * q + 2] * upper[EDGE : EDGE + step]
            centre += taps[6 * q + 4] * value
            for k in range(LEVELS):
                here = levels[q] == k + 1
                behind[k] += jnp.where(here, taps[6 * q + 3], 0.0) * value
                ahead[k] += jnp.where(here, taps[6 * q + 5], 0.0) * value
        out[c, pl.ds(row, step), :] = centre
        for k in range(LEVELS):
            plus[k, c, pl.ds(row, step), :] = ahead[k]
            minus[k, c, pl.ds(row, step), :] = behind[k]
        return carry

    lax.fori_loop(0, channels * (tall // step), one, 0)
    lane = lane_index(cols)
    near = lane_index(LANES)
    right = jnp.zeros((tall, LANES), F32)
    left = jnp.zeros((tall, LANES), F32)
    for c in range(channels):
        total = out[c]
        to_right = jnp.zeros((tall, LANES), F32)
        to_left = jnp.zeros((tall, LANES), F32)
        for level in range(LEVELS):
            gap = 2**level
            moved = turned(plus[level, c], gap)
            total += jnp.where(lane >= gap, moved, 0.0)
            to_right += jnp.where(near < gap, moved[:, :LANES], 0.0)
            moved = turned(minus[level, c], -gap)
            total += jnp.where(lane < cols - gap, moved, 0.0)
            to_left += jnp.where(near >= LANES - gap, moved[:, cols - LANES :], 0.0)
        out[c] = total
        right += turned(to_right, HALO * c)
        left += turned(to_left, -HALO * c)
    spill_right[...] = right
    spill_left[...] = left


def widen(tile, cols, at_end):
    if cols == LANES:
        return tile
    rest = jnp.zeros((tile.shape[0], cols - LANES), F32)
    return jnp.concatenate([rest, tile] if at_end else [tile, rest], axis=1)


def update_body(
    now, gradient, synth, side_low, side_high, top, bottom, updated, leading, pack_left, pack_right
):
    channels, rows, cols = now.shape
    near = lane_index(LANES)
    to_left = jnp.zeros((rows, LANES), F32)
    to_right = jnp.zeros((rows, LANES), F32)
    none = jnp.zeros((rows - EDGE, cols), F32)

    def folded(side):
        inside = side[EDGE : EDGE + rows, :]
        rest = jnp.zeros((rows - EDGE, LANES), F32)
        inside += jnp.concatenate([side[:EDGE, :], rest], axis=0)
        inside += jnp.concatenate([rest, side[EDGE + rows :, :]], axis=0)
        return inside

    low = folded(side_low)
    high = folded(side_high)
    for c in range(channels):
        total = synth[c, EDGE : EDGE + rows, :]
        total += jnp.concatenate([top[c], none], axis=0)
        total += jnp.concatenate([none, bottom[c]], axis=0)
        total += widen(jnp.where(near < HALO, turned(low, -HALO * c), 0.0), cols, False)
        total += widen(jnp.where(near >= LANES - HALO, turned(high, HALO * c), 0.0), cols, True)
        before = now[c]
        after = jnp.maximum(before - STEP_PRIMAL * (gradient[c] + total), 0.0)
        updated[c] = after
        ahead = 2.0 * after - before
        leading[c] = ahead
        to_left += turned(jnp.where(near < HALO, ahead[:, :LANES], 0.0), HALO * c)
        to_right += turned(
            jnp.where(near >= LANES - HALO, ahead[:, cols - LANES :], 0.0), -HALO * c
        )
    for pack, value in ((pack_left, to_left), (pack_right, to_right)):
        pack[0:EDGE, :] = value[:EDGE]
        pack[EDGE : EDGE + rows, :] = value
        pack[EDGE + rows :, :] = value[rows - EDGE :]


def analysis_body(
    leading, side_low, side_high, top, bottom, dual, taps, levels, radius, out, fields
):
    bases, channels, rows, cols = dual.shape
    near = lane_index(LANES)
    for c in range(channels):
        field = jnp.concatenate([top[c], leading[c], bottom[c]], axis=0)
        before = turned(side_low, HALO * c)
        behind = turned(side_high, -HALO * c)
        fields[0, c] = field[EDGE : EDGE + rows]
        for level in range(LEVELS):
            gap = 2**level
            moved = turned(field, gap)
            first = jnp.where(near < gap, turned(before, gap), moved[:, :LANES])
            if cols > LANES:
                first = jnp.concatenate([first, moved[:, LANES:]], axis=1)
            moved = turned(field, -gap)
            last = jnp.where(near >= LANES - gap, turned(behind, -gap), moved[:, cols - LANES :])
            if cols > LANES:
                last = jnp.concatenate([moved[:, : cols - LANES], last], axis=1)
            place = 8 * level
            for down in (-gap, 0, gap):
                for shifted in (first, field, last):
                    if down or shifted is not field:
                        place += 1
                        fields[place, c] = shifted[EDGE + down : EDGE + down + rows]

    def one(i, carry):
        q = lax.div(i, rows // EDGE)
        row = pl.ds(pl.multiple_of(lax.rem(i, rows // EDGE) * EDGE, EDGE), EDGE)
        place = 8 * (jnp.clip(levels[q], 1, LEVELS) - 1)
        weights = [
            (STEP_DUAL * taps[6 * q + a]) * taps[6 * q + 3 + e] for a in range(3) for e in range(3)
        ]
        raised = []
        energy = jnp.zeros((EDGE, cols), F32)
        for c in range(channels):
            value = dual[q, c, row, :] + weights[4] * fields[0, c, row, :]
            for j, weight in enumerate(weights[:4] + weights[5:]):
                value += weight * fields[place + 1 + j, c, row, :]
            energy += value * value
            raised.append(value)
        factor = radius[q] / jnp.maximum(jnp.sqrt(energy), radius[q])
        for c in range(channels):
            out[q, c, row, :] = raised[c] * factor
        return carry

    lax.fori_loop(0, bases * (rows // EDGE), one, 0, unroll=2)


MESH = pl.DeviceIdType.MESH


def forward_chunk(block, at, cos_ref, sin_ref, g_high, g_low, r_ref, total):
    picked = r_ref.shape[0] // 4

    def rows_of(screen):
        high, low = halves(block * screen[:, at])
        both = dot(r_ref[...], high)
        return both[: 2 * picked] + both[2 * picked :] + dot(r_ref[0 : 2 * picked, :], low)

    real = rows_of(cos_ref)
    imag = rows_of(sin_ref)
    spectrum = jnp.concatenate(
        [real[:picked] - imag[picked:], imag[:picked] + real[picked:]], axis=0
    )
    total[...] += dot_three(spectrum, g_high[at, :], g_low[at, :])


def misfit_of(total, data):
    picked, vis = data.shape[1:]
    sums = total[...]
    real = sums[:picked, :vis] - sums[picked:, vis:] - data[0]
    imag = sums[:picked, vis:] + sums[picked:, :vis] - data[1]
    total[...] = jnp.concatenate(
        [jnp.concatenate([real, imag], axis=1), jnp.concatenate([imag, -real], axis=1)], axis=0
    )


def backward_chunk(misfit, at, cos_ref, sin_ref, g_high, g_low, rt_ref):
    picked = misfit.shape[0] // 2
    back = dot_three(misfit, g_high[at, :], g_low[at, :], True)
    swapped = jnp.concatenate([back[picked:], -back[:picked]], axis=0)
    high, low = halves(jnp.concatenate([back, swapped], axis=1))
    grid = dot(rt_ref[...], jnp.concatenate([high, low, high], axis=0))
    chunk = back.shape[1]
    return cos_ref[:, at] * grid[:, :chunk] + sin_ref[:, at] * grid[:, chunk:]


def whole_body(
    nc,
    nt,
    sky,
    dual,
    phase,
    rows_col,
    rows_lane,
    weight,
    data,
    taps,
    levels,
    radius,
    sky_out,
    dual_out,
    cos_ref,
    sin_ref,
    g_high,
    g_low,
    r_ref,
    rt_ref,
    slabs,
    total,
    image,
    part,
    pair,
    strip,
    summed,
    gradient,
    sky_mid,
    dual_mid,
    synth,
    padded,
    plus,
    minus,
    leading,
    fields,
    side_low,
    side_high,
    top,
    bottom,
    pack_right,
    pack_left,
    edge_top,
    edge_bottom,
    a_send,
    a_recv,
    b_send,
    b_recv,
    c_send,
    c_recv,
    p_send,
    p_recv,
    s_send,
    s_recv,
    z_send,
    z_recv,
    h_send,
    h_recv,
):
    channels, rows, cols = sky.shape
    tall = rows + 2 * EDGE
    chips = nt // 2
    c = lax.axis_index("chan")
    t = lax.axis_index("tblk")
    core = lax.rem(t, 2)
    chip = lax.div(t, 2)
    right, left = lax.rem(c + 1, nc), lax.rem(c + nc - 1, nc)
    below, above = lax.rem(t + 1, nt), lax.rem(t + nt - 1, nt)
    sibling = (c, 2 * chip + 1 - core)

    def plane(distance):
        return 2 * lax.rem(chip + distance, chips) + core

    partners = [(lax.rem(c + d, nc), t) for d in range(1, nc)]
    partners += [(c, plane(d)) for d in range(1, chips)]
    partners += [(c, below), (c, above)]
    partners += [(right, below), (right, above), (left, below), (left, above)]
    barrier = pltpu.get_barrier_semaphore()
    for partner in partners:
        pl.semaphore_signal(barrier, inc=1, device_id=partner, device_id_type=MESH)
    pl.semaphore_wait(barrier, len(partners))

    def remote(src, dst, send, recv, device):
        return pltpu.make_async_remote_copy(
            src_ref=src,
            dst_ref=dst,
            send_sem=send,
            recv_sem=recv,
            device_id=device,
            device_id_type=MESH,
        )

    def strip_of(owner):
        return pl.ds(pl.multiple_of(owner * rows, rows), rows)

    def column(k):
        return lax.rem(c + k, nc)

    def tile_to_channel(it, source, k):
        target = column(k)
        return remote(
            source.at[target],
            image.at[it, c, strip_of(t), :],
            a_send.at[it, k],
            a_recv.at[it, nc - k],
            (target, t),
        )

    def tile_from_channel(it, source, k):
        other = column(k)
        return remote(
            source.at[other],
            image.at[it, other, strip_of(t), :],
            a_send.at[it, k],
            a_recv.at[it, k],
            (other, t),
        )

    def tile_to_chip(it, d, k):
        where = image.at[it, column(k), strip_of(t), :]
        return remote(
            where, where, b_send.at[it, d - 1, k], b_recv.at[it, d - 1, k], (c, plane(d))
        )

    def tile_to_sibling(it, d, k):
        where = image.at[it, column(k), strip_of(plane(chips - d)), :]
        return remote(where, where, c_send.at[it, d, k], c_recv.at[it, d, k], sibling)

    def half_to_sibling(it, k):
        return remote(
            part.at[k, 1 - core], pair.at[it, k], p_send.at[it, k], p_recv.at[it, k], sibling
        )

    def strip_to_chip(it, d, k):
        return remote(
            part.at[k, core, lax.rem(chip + d, chips)],
            strip.at[it, d - 1, k],
            s_send.at[it, d - 1, k],
            s_recv.at[it, d - 1, k],
            (c, plane(d)),
        )

    def tile_to_facet(it, k):
        target = column(k)
        return remote(
            summed.at[it, k],
            gradient.at[it, c],
            z_send.at[it, k],
            z_recv.at[it, nc - k],
            (target, t),
        )

    def tile_from_facet(it, k):
        other = column(k)
        return remote(
            summed.at[it, k],
            gradient.at[it, other],
            z_send.at[it, k],
            z_recv.at[it, k],
            (other, t),
        )

    first, middle, last = pl.ds(0, EDGE), pl.ds(EDGE, rows), pl.ds(EDGE + rows, EDGE)

    def edges(stage):
        routes = [
            (pack_right.at[stage, middle], side_low.at[stage, middle], (right, t)),
            (pack_right.at[stage, last], side_low.at[stage, first], (right, below)),
            (pack_right.at[stage, first], side_low.at[stage, last], (right, above)),
            (pack_left.at[stage, middle], side_high.at[stage, middle], (left, t)),
            (pack_left.at[stage, last], side_high.at[stage, first], (left, below)),
            (pack_left.at[stage, first], side_high.at[stage, last], (left, above)),
            (edge_bottom.at[stage], top.at[stage], (c, below)),
            (edge_top.at[stage], bottom.at[stage], (c, above)),
        ]
        return [
            remote(src, dst, h_send.at[stage, i], h_recv.at[stage, i], device)
            for i, (src, dst, device) in enumerate(routes)
        ]

    def kept(flag, value):
        return jnp.where(flag, value, jnp.zeros_like(value))

    def side_of(ref, stage, inside):
        return jnp.concatenate(
            [
                kept(inside & (t > 0), ref[stage, 0:EDGE, :]),
                kept(inside, ref[stage, EDGE : EDGE + rows, :]),
                kept(inside & (t < nt - 1), ref[stage, EDGE + rows :, :]),
            ],
            axis=0,
        )

    def arrived(stage):
        for copy in edges(stage):
            copy.wait()
        return (
            side_of(side_low, stage, c > 0),
            side_of(side_high, stage, c < nc - 1),
            [kept(t > 0, top[stage, i]) for i in range(channels)],
            [kept(t < nt - 1, bottom[stage, i]) for i in range(channels)],
        )

    now, coefs = sky, dual
    for it in range(ITERS):
        next_sky, next_dual = (sky_out, dual_out) if it == ITERS - 1 else (sky_mid, dual_mid)
        for k in range(1, nc):
            tile_to_channel(it, now, k).start()
        image[it, c, strip_of(t), :] = now[c]
        if it == 0:
            screens(phase, cos_ref, sin_ref)
        for k in range(nc):
            if k > 0:
                tile_from_channel(it, now, k).wait_recv()
            for d in range(1, chips):
                tile_to_chip(it, d, k).start()
            tile_to_sibling(it, 0, k).start()
        if it == 0:
            transforms(weight, rows_col, rows_lane, g_high, g_low, r_ref, rt_ref, slabs)
        synthesis_body(
            coefs,
            taps,
            levels,
            synth,
            pack_right.at[2 * it],
            pack_left.at[2 * it],
            padded,
            plus,
            minus,
        )
        edge_top[2 * it] = synth[:, 0:EDGE, :]
        edge_bottom[2 * it] = synth[:, EDGE + rows :, :]
        for k in range(nc):
            for d in range(1, chips):
                tile_to_chip(it, d, k).wait_recv()
                tile_to_sibling(it, d, k).start()
        for copy in edges(2 * it):
            copy.start()

        total[...] = jnp.zeros_like(total)
        for k in range(nc):
            for d in range(chips):
                tile_to_sibling(it, d, k).wait_recv()

        def forward(k, carry):
            here = column(k)
            at = pl.ds(pl.multiple_of(here * cols, cols), cols)
            forward_chunk(image[it, here], at, cos_ref, sin_ref, g_high, g_low, r_ref, total)
            return carry

        lax.fori_loop(0, nc, forward, 0)
        misfit_of(total, data)

        def backward(step, carry):
            @pl.when(step < nc)
            def _():
                k = lax.rem(step + 1, nc)
                at = pl.ds(pl.multiple_of(column(k) * cols, cols), cols)
                value = backward_chunk(total[...], at, cos_ref, sin_ref, g_high, g_low, rt_ref)
                for owner in range(nt):
                    part[k, owner % 2, owner // 2] = value[owner * rows : (owner + 1) * rows]
                half_to_sibling(it, k).start()

            @pl.when((step >= 1) & (step <= nc))
            def _():
                k = lax.rem(step, nc)
                half_to_sibling(it, k).wait_recv()
                part[k, core] += pair[it, k]
                for d in range(1, chips):
                    strip_to_chip(it, d, k).start()

            @pl.when(step >= 2)
            def _():
                k = lax.rem(step - 1, nc)
                value = part[k, core, chip]
                for d in range(1, chips):
                    strip_to_chip(it, d, k).wait_recv()
                    value += strip[it, d - 1, k]

                @pl.when(k > 0)
                def _():
                    summed[it, k] = value
                    tile_to_facet(it, k).start()

                @pl.when(k == 0)
                def _():
                    gradient[it, c] = value

            return carry

        lax.fori_loop(0, nc + 2, backward, 0)
        low, high, up, down = arrived(2 * it)
        for k in range(1, nc):
            tile_from_facet(it, k).wait_recv()
        stage = 2 * it + 1
        update_body(
            now,
            gradient.at[it],
            synth,
            low,
            high,
            up,
            down,
            next_sky,
            leading,
            pack_left.at[stage],
            pack_right.at[stage],
        )
        edge_top[stage] = leading[:, 0:EDGE, :]
        edge_bottom[stage] = leading[:, rows - EDGE :, :]
        for copy in edges(stage):
            copy.start()
        low, high, up, down = arrived(stage)
        analysis_body(
            leading, low, high, up, down, coefs, taps, levels, radius, next_dual, fields
        )
        for k in range(nc):
            half_to_sibling(it, k).wait_send()
            for d in range(1, chips):
                tile_to_chip(it, d, k).wait_send()
                strip_to_chip(it, d, k).wait_send()
            for d in range(chips):
                tile_to_sibling(it, d, k).wait_send()
            if k > 0:
                tile_to_channel(it, now, k).wait_send()
                tile_to_facet(it, k).wait_send()
        now, coefs = next_sky, next_dual


def arr(*shape, dtype=F32):
    return jax.ShapeDtypeStruct(shape, dtype)


def per_device(sky, dual, phase, rows_at, weight, vis_data, filters, level_counts, radius):
    channels, rows, cols = sky.shape
    nc, nt = lax.axis_size("chan"), lax.axis_size("tblk")
    chips = nt // 2
    full_rows, full_cols = phase.shape[2:]
    vis = weight.shape[3]
    picked = rows_at.shape[2]
    tall = rows + 2 * EDGE
    stages = 2 * ITERS
    block = lambda *shape, dtype=F32: pltpu.VMEM(shape, dtype)
    scratch = [
        block(full_rows, full_cols),
        block(full_rows, full_cols),
        block(full_cols, 2 * vis, dtype=BF16),
        block(full_cols, 2 * vis, dtype=BF16),
        block(4 * picked, full_rows, dtype=BF16),
        block(full_rows, 6 * picked, dtype=BF16),
        block(vis // LANES, full_cols, LANES),
        block(2 * picked, 2 * vis),
        block(ITERS, nc, full_rows, cols),
        block(nc, 2, chips, rows, cols),
        block(ITERS, nc, chips, rows, cols),
        block(ITERS, chips - 1, nc, rows, cols),
        block(ITERS, nc, rows, cols),
        block(ITERS, channels, rows, cols),
        block(*sky.shape),
        block(*dual.shape),
        block(channels, tall, cols),
        block(*dual.shape[:2], rows + 4 * EDGE, cols),
        block(LEVELS, channels, tall, cols),
        block(LEVELS, channels, tall, cols),
        block(*sky.shape),
        block(1 + 8 * LEVELS, channels, rows, cols),
        block(stages, tall, LANES),
        block(stages, tall, LANES),
        block(stages, channels, EDGE, cols),
        block(stages, channels, EDGE, cols),
        block(stages, tall, LANES),
        block(stages, tall, LANES),
        block(stages, channels, EDGE, cols),
        block(stages, channels, EDGE, cols),
    ]
    for shape in (
        (ITERS, nc),
        (ITERS, chips - 1, nc),
        (ITERS, chips, nc),
        (ITERS, nc),
        (ITERS, chips - 1, nc),
        (ITERS, nc),
        (stages, 8),
    ):
        scratch += [pltpu.SemaphoreType.DMA(shape)] * 2
    return pl.pallas_call(
        functools.partial(whole_body, nc, nt),
        out_shape=(arr(*sky.shape), arr(*dual.shape)),
        in_specs=[VMEM] * 7 + [SMEM] * 3,
        out_specs=(VMEM, VMEM),
        scratch_shapes=scratch,
        compiler_params=pltpu.CompilerParams(
            vmem_limit_bytes=60 * 1024 * 1024, collective_id=0, has_side_effects=True
        ),
        name="primal_dual",
    )(
        sky,
        dual,
        phase[0, 0],
        rows_at[0, 0][:, None],
        rows_at[0, 0][None, :],
        weight[0, 0],
        vis_data[0, 0],
        filters.reshape(-1),
        level_counts,
        radius,
    )


def solution(mesh):
    placed = (
        P(None, "tblk", "chan"),
        P(None, None, "tblk", "chan"),
        P("chan", "tblk", None, None),
        P("chan", "tblk", None),
        P("chan", "tblk", None, None),
        P("chan", "tblk", None, None, None),
        P(),
        P(),
        P(),
    )
    return jax.shard_map(
        per_device,
        mesh=mesh,
        in_specs=placed,
        out_specs=(P(None, "tblk", "chan"), P(None, None, "tblk", "chan")),
        check_vma=False,
    )
```

```python
import functools
import math

import jax
import jax.numpy as jnp
from jax import lax
from jax.experimental import pallas as pl
from jax.experimental.pallas import tpu as pltpu
from jax.sharding import PartitionSpec as P

ITERS = 2
HALO = 4
EDGE = 8
LANES = 128
LEVELS = 3
STEP_PRIMAL = 0.5
STEP_DUAL = 0.5
F32 = jnp.float32
BF16 = jnp.bfloat16
VMEM = pl.BlockSpec(memory_space=pltpu.VMEM)
SMEM = pl.BlockSpec(memory_space=pltpu.SMEM)


def sincos(angle):
    turn = jnp.floor(angle * (2.0 / math.pi) + 0.5)
    rest = angle - turn * 1.5703125
    rest = rest - turn * 4.83751296997e-04
    rest = rest - turn * 7.54978995489e-08
    square = rest * rest
    sine = rest + rest * square * (
        -1.6666654611e-1 + square * (8.3321608736e-3 - square * 1.9515295891e-4)
    )
    cosine = (1.0 - 0.5 * square) + square * square * (
        4.166664568298827e-2 + square * (-1.388731625493765e-3 + square * 2.443315711809948e-5)
    )
    odd = jnp.abs(turn) == 1.0
    far = jnp.abs(turn) == 2.0
    sin_out = jnp.where(odd, turn * cosine, jnp.where(far, -sine, sine))
    cos_out = jnp.where(odd, -turn * sine, jnp.where(far, -cosine, cosine))
    return sin_out, cos_out


def root_of_unity(number, count):
    number = lax.rem(number, jnp.int32(count))
    number = jnp.where(number >= count // 2, number - count, number)
    return sincos(number.astype(F32) * (2.0 * math.pi / count))


def halves(value):
    high = value.astype(BF16)
    return high, (value - high.astype(F32)).astype(BF16)


def dot(left, right, transposed=False):
    dims = (((1,), (1 if transposed else 0,)), ((), ()))
    return lax.dot_general(left, right, dims, preferred_element_type=F32)


def dot_three(left, right_high, right_low, transposed=False):
    rows = left.shape[0]
    high, low = halves(left)
    both = dot(jnp.concatenate([high, low], axis=0), right_high, transposed)
    return both[:rows] + both[rows:] + dot(high, right_low, transposed)


def screens(phase, cos_ref, sin_ref):
    step = 16

    def screen(i, carry):
        at = pl.ds(pl.multiple_of(i * step, step), step)
        sine, cosine = sincos(phase[at, :])
        cos_ref[at, :] = cosine
        sin_ref[at, :] = sine
        return carry

    lax.fori_loop(0, phase.shape[0] // step, screen, 0)


def transforms(weight, rows_col, rows_lane, g_high, g_low, r_ref, rt_ref, slabs):
    full_rows = rt_ref.shape[0]
    full_cols, vis = weight.shape
    picked = rows_col.shape[0]
    sine, cosine = root_of_unity(
        rows_col[:, 0:1] * lax.broadcasted_iota(jnp.int32, (picked, full_rows), 1), full_rows
    )
    scale = 1.0 / math.sqrt(full_rows)
    high, low = halves(jnp.concatenate([cosine * scale, -sine * scale], axis=0))
    r_ref[...] = jnp.concatenate([high, low], axis=0)
    sine, cosine = root_of_unity(
        rows_lane[0:1, :] * lax.broadcasted_iota(jnp.int32, (full_rows, picked), 0), full_rows
    )
    high, low = halves(jnp.concatenate([cosine * scale, -sine * scale], axis=1))
    rt_ref[...] = jnp.concatenate([high, high, low], axis=1)

    half = full_cols // 2
    scale = 1.0 / math.sqrt(full_cols)
    count = vis // LANES
    for k in range(count):
        slabs[k] = weight[:, k * LANES : (k + 1) * LANES] * scale
    even_high, even_low = halves(
        jnp.concatenate([slabs[k, pl.ds(0, half, 2), :] for k in range(count)], axis=1)
    )
    odd_high, odd_low = halves(
        jnp.concatenate([slabs[k, pl.ds(1, half, 2), :] for k in range(count)], axis=1)
    )
    tile = 64

    def transform(i, carry):
        base = pl.multiple_of(i * tile, tile)
        line = base + lax.broadcasted_iota(jnp.int32, (tile, half), 0)
        cell = 2 * lax.broadcasted_iota(jnp.int32, (tile, half), 1)
        sine, cosine = root_of_unity(line * cell, full_cols)
        even = dot_three(jnp.concatenate([cosine, -sine], axis=0), even_high, even_low)
        sine, cosine = root_of_unity(line * (cell + 1), full_cols)
        odd = dot_three(jnp.concatenate([cosine, -sine], axis=0), odd_high, odd_low)
        for where, total in ((base, even + odd), (base + half, even - odd)):
            where = pl.multiple_of(where, tile)
            high, low = halves(jnp.concatenate([total[:tile], total[tile:]], axis=1))
            g_high[pl.ds(where, tile), :] = high
            g_low[pl.ds(where, tile), :] = low
        return carry

    lax.fori_loop(0, half // tile, transform, 0)


def lane_index(width):
    return lax.broadcasted_iota(jnp.int32, (1, width), 1)


def turned(value, distance):
    distance = distance % value.shape[-1]
    return value if distance == 0 else pltpu.roll(value, distance, value.ndim - 1)


def gap_of(level):
    return level + jnp.where(level == LEVELS, 1, 0)


def synthesis_body(dual, taps, levels, out, spill_right, spill_left, padded, plus, minus):
    bases, channels, rows, cols = dual.shape
    tall = rows + 2 * EDGE
    step = 16
    zeros = jnp.zeros((bases, channels, 2 * EDGE, cols), F32)
    padded[:, :, : 2 * EDGE, :] = zeros
    padded[:, :, rows + 2 * EDGE :, :] = zeros
    padded[:, :, 2 * EDGE : 2 * EDGE + rows, :] = dual[...]

    def one(i, carry):
        c = lax.rem(i, channels)
        row = pl.multiple_of(lax.div(i, channels) * step, step)
        none = jnp.zeros((step, cols), F32)
        centre, ahead, behind = none, [none] * LEVELS, [none] * LEVELS
        for q in range(bases):
            gap = gap_of(levels[q])
            block = padded[q, c, pl.ds(row, step + 2 * EDGE), :]
            value = taps[6 * q + 1] * block[EDGE : EDGE + step]
            lower = pltpu.roll(block, step + 2 * EDGE - gap, 0)
            value += taps[6 * q] * lower[EDGE : EDGE + step]
            upper = pltpu.roll(block, gap, 0)
            value += taps[6 * q + 2] * upper[EDGE : EDGE + step]
            centre += taps[6 * q + 4] * value
            for k in range(LEVELS):
                here = levels[q] == k + 1
                behind[k] += jnp.where(here, taps[6 * q + 3], 0.0) * value
                ahead[k] += jnp.where(here, taps[6 * q + 5], 0.0) * value
        out[c, pl.ds(row, step), :] = centre
        for k in range(LEVELS):
            plus[k, c, pl.ds(row, step), :] = ahead[k]
            minus[k, c, pl.ds(row, step), :] = behind[k]
        return carry

    lax.fori_loop(0, channels * (tall // step), one, 0)
    lane = lane_index(cols)
    near = lane_index(LANES)
    right = jnp.zeros((tall, LANES), F32)
    left = jnp.zeros((tall, LANES), F32)
    for c in range(channels):
        total = out[c]
        to_right = jnp.zeros((tall, LANES), F32)
        to_left = jnp.zeros((tall, LANES), F32)
        for level in range(LEVELS):
            gap = 2**level
            moved = turned(plus[level, c], gap)
            total += jnp.where(lane >= gap, moved, 0.0)
            to_right += jnp.where(near < gap, moved[:, :LANES], 0.0)
            moved = turned(minus[level, c], -gap)
            total += jnp.where(lane < cols - gap, moved, 0.0)
            to_left += jnp.where(near >= LANES - gap, moved[:, cols - LANES :], 0.0)
        out[c] = total
        right += turned(to_right, HALO * c)
        left += turned(to_left, -HALO * c)
    spill_right[...] = right
    spill_left[...] = left


def widen(tile, cols, at_end):
    if cols == LANES:
        return tile
    rest = jnp.zeros((tile.shape[0], cols - LANES), F32)
    return jnp.concatenate([rest, tile] if at_end else [tile, rest], axis=1)


def update_body(
    now, gradient, synth, side_low, side_high, top, bottom, updated, leading, pack_left, pack_right
):
    channels, rows, cols = now.shape
    near = lane_index(LANES)
    to_left = jnp.zeros((rows, LANES), F32)
    to_right = jnp.zeros((rows, LANES), F32)
    none = jnp.zeros((rows - EDGE, cols), F32)

    def folded(side):
        inside = side[EDGE : EDGE + rows, :]
        rest = jnp.zeros((rows - EDGE, LANES), F32)
        inside += jnp.concatenate([side[:EDGE, :], rest], axis=0)
        inside += jnp.concatenate([rest, side[EDGE + rows :, :]], axis=0)
        return inside

    low = folded(side_low)
    high = folded(side_high)
    for c in range(channels):
        total = synth[c, EDGE : EDGE + rows, :]
        total += jnp.concatenate([top[c], none], axis=0)
        total += jnp.concatenate([none, bottom[c]], axis=0)
        total += widen(jnp.where(near < HALO, turned(low, -HALO * c), 0.0), cols, False)
        total += widen(jnp.where(near >= LANES - HALO, turned(high, HALO * c), 0.0), cols, True)
        before = now[c]
        after = jnp.maximum(before - STEP_PRIMAL * (gradient[c] + total), 0.0)
        updated[c] = after
        ahead = 2.0 * after - before
        leading[c] = ahead
        to_left += turned(jnp.where(near < HALO, ahead[:, :LANES], 0.0), HALO * c)
        to_right += turned(
            jnp.where(near >= LANES - HALO, ahead[:, cols - LANES :], 0.0), -HALO * c
        )
    for pack, value in ((pack_left, to_left), (pack_right, to_right)):
        pack[0:EDGE, :] = value[:EDGE]
        pack[EDGE : EDGE + rows, :] = value
        pack[EDGE + rows :, :] = value[rows - EDGE :]


def analysis_body(
    leading, side_low, side_high, top, bottom, dual, taps, levels, radius, out, fields
):
    bases, channels, rows, cols = dual.shape
    near = lane_index(LANES)
    for c in range(channels):
        field = jnp.concatenate([top[c], leading[c], bottom[c]], axis=0)
        before = turned(side_low, HALO * c)
        behind = turned(side_high, -HALO * c)
        fields[0, c] = field[EDGE : EDGE + rows]
        for level in range(LEVELS):
            gap = 2**level
            moved = turned(field, gap)
            first = jnp.where(near < gap, turned(before, gap), moved[:, :LANES])
            if cols > LANES:
                first = jnp.concatenate([first, moved[:, LANES:]], axis=1)
            moved = turned(field, -gap)
            last = jnp.where(near >= LANES - gap, turned(behind, -gap), moved[:, cols - LANES :])
            if cols > LANES:
                last = jnp.concatenate([moved[:, : cols - LANES], last], axis=1)
            place = 8 * level
            for down in (-gap, 0, gap):
                for shifted in (first, field, last):
                    if down or shifted is not field:
                        place += 1
                        fields[place, c] = shifted[EDGE + down : EDGE + down + rows]

    def one(i, carry):
        q = lax.div(i, rows // EDGE)
        row = pl.ds(pl.multiple_of(lax.rem(i, rows // EDGE) * EDGE, EDGE), EDGE)
        place = 8 * (jnp.clip(levels[q], 1, LEVELS) - 1)
        weights = [
            (STEP_DUAL * taps[6 * q + a]) * taps[6 * q + 3 + e] for a in range(3) for e in range(3)
        ]
        raised = []
        energy = jnp.zeros((EDGE, cols), F32)
        for c in range(channels):
            value = dual[q, c, row, :] + weights[4] * fields[0, c, row, :]
            for j, weight in enumerate(weights[:4] + weights[5:]):
                value += weight * fields[place + 1 + j, c, row, :]
            energy += value * value
            raised.append(value)
        factor = radius[q] / jnp.maximum(jnp.sqrt(energy), radius[q])
        for c in range(channels):
            out[q, c, row, :] = raised[c] * factor
        return carry

    lax.fori_loop(0, bases * (rows // EDGE), one, 0, unroll=2)


MESH = pl.DeviceIdType.MESH


def forward_chunk(block, at, cos_ref, sin_ref, g_high, g_low, r_ref, total):
    picked = r_ref.shape[0] // 4

    def rows_of(screen):
        high, low = halves(block * screen[:, at])
        both = dot(r_ref[...], high)
        return both[: 2 * picked] + both[2 * picked :] + dot(r_ref[0 : 2 * picked, :], low)

    real = rows_of(cos_ref)
    imag = rows_of(sin_ref)
    spectrum = jnp.concatenate(
        [real[:picked] - imag[picked:], imag[:picked] + real[picked:]], axis=0
    )
    total[...] += dot_three(spectrum, g_high[at, :], g_low[at, :])


def misfit_of(total, data):
    picked, vis = data.shape[1:]
    sums = total[...]
    real = sums[:picked, :vis] - sums[picked:, vis:] - data[0]
    imag = sums[:picked, vis:] + sums[picked:, :vis] - data[1]
    total[...] = jnp.concatenate(
        [jnp.concatenate([real, imag], axis=1), jnp.concatenate([imag, -real], axis=1)], axis=0
    )


def backward_chunk(misfit, at, cos_ref, sin_ref, g_high, g_low, rt_ref):
    picked = misfit.shape[0] // 2
    back = dot_three(misfit, g_high[at, :], g_low[at, :], True)
    swapped = jnp.concatenate([back[picked:], -back[:picked]], axis=0)
    high, low = halves(jnp.concatenate([back, swapped], axis=1))
    grid = dot(rt_ref[...], jnp.concatenate([high, low, high], axis=0))
    chunk = back.shape[1]
    return cos_ref[:, at] * grid[:, :chunk] + sin_ref[:, at] * grid[:, chunk:]


def whole_body(
    nc,
    nt,
    sky,
    dual,
    phase,
    rows_col,
    rows_lane,
    weight,
    data,
    taps,
    levels,
    radius,
    sky_out,
    dual_out,
    cos_ref,
    sin_ref,
    g_high,
    g_low,
    r_ref,
    rt_ref,
    slabs,
    total,
    image,
    part,
    pair,
    strip,
    summed,
    gradient,
    sky_mid,
    dual_mid,
    synth,
    padded,
    plus,
    minus,
    leading,
    fields,
    side_low,
    side_high,
    top,
    bottom,
    pack_right,
    pack_left,
    edge_top,
    edge_bottom,
    a_send,
    a_recv,
    b_send,
    b_recv,
    c_send,
    c_recv,
    p_send,
    p_recv,
    s_send,
    s_recv,
    z_send,
    z_recv,
    h_send,
    h_recv,
):
    channels, rows, cols = sky.shape
    tall = rows + 2 * EDGE
    chips = nt // 2
    c = lax.axis_index("chan")
    t = lax.axis_index("tblk")
    core = lax.rem(t, 2)
    chip = lax.div(t, 2)
    right, left = lax.rem(c + 1, nc), lax.rem(c + nc - 1, nc)
    below, above = lax.rem(t + 1, nt), lax.rem(t + nt - 1, nt)
    sibling = (c, 2 * chip + 1 - core)

    def plane(distance):
        return 2 * lax.rem(chip + distance, chips) + core

    partners = [(lax.rem(c + d, nc), t) for d in range(1, nc)]
    partners += [(c, plane(d)) for d in range(1, chips)]
    partners += [(c, below), (c, above)]
    partners += [(right, below), (right, above), (left, below), (left, above)]
    barrier = pltpu.get_barrier_semaphore()
    for partner in partners:
        pl.semaphore_signal(barrier, inc=1, device_id=partner, device_id_type=MESH)
    pl.semaphore_wait(barrier, len(partners))

    def remote(src, dst, send, recv, device):
        return pltpu.make_async_remote_copy(
            src_ref=src,
            dst_ref=dst,
            send_sem=send,
            recv_sem=recv,
            device_id=device,
            device_id_type=MESH,
        )

    def strip_of(owner):
        return pl.ds(pl.multiple_of(owner * rows, rows), rows)

    def column(k):
        return lax.rem(c + k, nc)

    def tile_to_channel(it, source, k):
        target = column(k)
        return remote(
            source.at[target],
            image.at[it, c, strip_of(t), :],
            a_send.at[it, k],
            a_recv.at[it, nc - k],
            (target, t),
        )

    def tile_from_channel(it, source, k):
        other = column(k)
        return remote(
            source.at[other],
            image.at[it, other, strip_of(t), :],
            a_send.at[it, k],
            a_recv.at[it, k],
            (other, t),
        )

    def tile_to_chip(it, d, k):
        where = image.at[it, column(k), strip_of(t), :]
        return remote(
            where, where, b_send.at[it, d - 1, k], b_recv.at[it, d - 1, k], (c, plane(d))
        )

    def tile_to_sibling(it, d, k):
        where = image.at[it, column(k), strip_of(plane(chips - d)), :]
        return remote(where, where, c_send.at[it, d, k], c_recv.at[it, d, k], sibling)

    def half_to_sibling(it, k):
        return remote(
            part.at[k, 1 - core], pair.at[it, k], p_send.at[it, k], p_recv.at[it, k], sibling
        )

    def strip_to_chip(it, d, k):
        return remote(
            part.at[k, core, lax.rem(chip + d, chips)],
            strip.at[it, d - 1, k],
            s_send.at[it, d - 1, k],
            s_recv.at[it, d - 1, k],
            (c, plane(d)),
        )

    def tile_to_facet(it, k):
        target = column(k)
        return remote(
            summed.at[it, k],
            gradient.at[it, c],
            z_send.at[it, k],
            z_recv.at[it, nc - k],
            (target, t),
        )

    def tile_from_facet(it, k):
        other = column(k)
        return remote(
            summed.at[it, k],
            gradient.at[it, other],
            z_send.at[it, k],
            z_recv.at[it, k],
            (other, t),
        )

    first, middle, last = pl.ds(0, EDGE), pl.ds(EDGE, rows), pl.ds(EDGE + rows, EDGE)

    def edges(stage):
        routes = [
            (pack_right.at[stage, middle], side_low.at[stage, middle], (right, t)),
            (pack_right.at[stage, last], side_low.at[stage, first], (right, below)),
            (pack_right.at[stage, first], side_low.at[stage, last], (right, above)),
            (pack_left.at[stage, middle], side_high.at[stage, middle], (left, t)),
            (pack_left.at[stage, last], side_high.at[stage, first], (left, below)),
            (pack_left.at[stage, first], side_high.at[stage, last], (left, above)),
            (edge_bottom.at[stage], top.at[stage], (c, below)),
            (edge_top.at[stage], bottom.at[stage], (c, above)),
        ]
        return [
            remote(src, dst, h_send.at[stage, i], h_recv.at[stage, i], device)
            for i, (src, dst, device) in enumerate(routes)
        ]

    def kept(flag, value):
        return jnp.where(flag, value, jnp.zeros_like(value))

    def side_of(ref, stage, inside):
        return jnp.concatenate(
            [
                kept(inside & (t > 0), ref[stage, 0:EDGE, :]),
                kept(inside, ref[stage, EDGE : EDGE + rows, :]),
                kept(inside & (t < nt - 1), ref[stage, EDGE + rows :, :]),
            ],
            axis=0,
        )

    def arrived(stage):
        for copy in edges(stage):
            copy.wait()
        return (
            side_of(side_low, stage, c > 0),
            side_of(side_high, stage, c < nc - 1),
            [kept(t > 0, top[stage, i]) for i in range(channels)],
            [kept(t < nt - 1, bottom[stage, i]) for i in range(channels)],
        )

    now, coefs = sky, dual
    for it in range(ITERS):
        next_sky, next_dual = (sky_out, dual_out) if it == ITERS - 1 else (sky_mid, dual_mid)
        for k in range(1, nc):
            tile_to_channel(it, now, k).start()
        image[it, c, strip_of(t), :] = now[c]
        for k in range(nc):
            if k > 0:
                tile_from_channel(it, now, k).wait_recv()
            for d in range(1, chips):
                tile_to_chip(it, d, k).start()
            tile_to_sibling(it, 0, k).start()
            if it == 0 and k == 0:
                screens(phase, cos_ref, sin_ref)
        if it == 0:
            transforms(weight, rows_col, rows_lane, g_high, g_low, r_ref, rt_ref, slabs)
        synthesis_body(
            coefs,
            taps,
            levels,
            synth,
            pack_right.at[2 * it],
            pack_left.at[2 * it],
            padded,
            plus,
            minus,
        )
        edge_top[2 * it] = synth[:, 0:EDGE, :]
        edge_bottom[2 * it] = synth[:, EDGE + rows :, :]
        for copy in edges(2 * it):
            copy.start()
        total[...] = jnp.zeros_like(total)

        def forward(step, carry):
            @pl.when(step < nc)
            def _():
                for d in range(1, chips):
                    tile_to_chip(it, d, step).wait_recv()
                    tile_to_sibling(it, d, step).start()

            @pl.when(step >= 1)
            def _():
                k = step - 1
                for d in range(chips):
                    tile_to_sibling(it, d, k).wait_recv()
                here = column(k)
                at = pl.ds(pl.multiple_of(here * cols, cols), cols)
                forward_chunk(image[it, here], at, cos_ref, sin_ref, g_high, g_low, r_ref, total)

            return carry

        lax.fori_loop(0, nc + 1, forward, 0)
        misfit_of(total, data)

        def backward(step, carry):
            @pl.when(step < nc)
            def _():
                k = lax.rem(step + 1, nc)
                at = pl.ds(pl.multiple_of(column(k) * cols, cols), cols)
                value = backward_chunk(total[...], at, cos_ref, sin_ref, g_high, g_low, rt_ref)
                for owner in range(nt):
                    part[k, owner % 2, owner // 2] = value[owner * rows : (owner + 1) * rows]
                half_to_sibling(it, k).start()

            @pl.when((step >= 1) & (step <= nc))
            def _():
                k = lax.rem(step, nc)
                half_to_sibling(it, k).wait_recv()
                part[k, core] += pair[it, k]
                for d in range(1, chips):
                    strip_to_chip(it, d, k).start()

            @pl.when(step >= 2)
            def _():
                k = lax.rem(step - 1, nc)
                value = part[k, core, chip]
                for d in range(1, chips):
                    strip_to_chip(it, d, k).wait_recv()
                    value += strip[it, d - 1, k]

                @pl.when(k > 0)
                def _():
                    summed[it, k] = value
                    tile_to_facet(it, k).start()

                @pl.when(k == 0)
                def _():
                    gradient[it, c] = value

            return carry

        lax.fori_loop(0, nc + 2, backward, 0)
        low, high, up, down = arrived(2 * it)
        for k in range(1, nc):
            tile_from_facet(it, k).wait_recv()
        stage = 2 * it + 1
        update_body(
            now,
            gradient.at[it],
            synth,
            low,
            high,
            up,
            down,
            next_sky,
            leading,
            pack_left.at[stage],
            pack_right.at[stage],
        )
        edge_top[stage] = leading[:, 0:EDGE, :]
        edge_bottom[stage] = leading[:, rows - EDGE :, :]
        for copy in edges(stage):
            copy.start()
        low, high, up, down = arrived(stage)
        analysis_body(
            leading, low, high, up, down, coefs, taps, levels, radius, next_dual, fields
        )
        for k in range(nc):
            half_to_sibling(it, k).wait_send()
            for d in range(1, chips):
                tile_to_chip(it, d, k).wait_send()
                strip_to_chip(it, d, k).wait_send()
            for d in range(chips):
                tile_to_sibling(it, d, k).wait_send()
            if k > 0:
                tile_to_channel(it, now, k).wait_send()
                tile_to_facet(it, k).wait_send()
        now, coefs = next_sky, next_dual


def arr(*shape, dtype=F32):
    return jax.ShapeDtypeStruct(shape, dtype)


def per_device(sky, dual, phase, rows_at, weight, vis_data, filters, level_counts, radius):
    channels, rows, cols = sky.shape
    nc, nt = lax.axis_size("chan"), lax.axis_size("tblk")
    chips = nt // 2
    full_rows, full_cols = phase.shape[2:]
    vis = weight.shape[3]
    picked = rows_at.shape[2]
    tall = rows + 2 * EDGE
    stages = 2 * ITERS
    block = lambda *shape, dtype=F32: pltpu.VMEM(shape, dtype)
    scratch = [
        block(full_rows, full_cols),
        block(full_rows, full_cols),
        block(full_cols, 2 * vis, dtype=BF16),
        block(full_cols, 2 * vis, dtype=BF16),
        block(4 * picked, full_rows, dtype=BF16),
        block(full_rows, 6 * picked, dtype=BF16),
        block(vis // LANES, full_cols, LANES),
        block(2 * picked, 2 * vis),
        block(ITERS, nc, full_rows, cols),
        block(nc, 2, chips, rows, cols),
        block(ITERS, nc, chips, rows, cols),
        block(ITERS, chips - 1, nc, rows, cols),
        block(ITERS, nc, rows, cols),
        block(ITERS, channels, rows, cols),
        block(*sky.shape),
        block(*dual.shape),
        block(channels, tall, cols),
        block(*dual.shape[:2], rows + 4 * EDGE, cols),
        block(LEVELS, channels, tall, cols),
        block(LEVELS, channels, tall, cols),
        block(*sky.shape),
        block(1 + 8 * LEVELS, channels, rows, cols),
        block(stages, tall, LANES),
        block(stages, tall, LANES),
        block(stages, channels, EDGE, cols),
        block(stages, channels, EDGE, cols),
        block(stages, tall, LANES),
        block(stages, tall, LANES),
        block(stages, channels, EDGE, cols),
        block(stages, channels, EDGE, cols),
    ]
    for shape in (
        (ITERS, nc),
        (ITERS, chips - 1, nc),
        (ITERS, chips, nc),
        (ITERS, nc),
        (ITERS, chips - 1, nc),
        (ITERS, nc),
        (stages, 8),
    ):
        scratch += [pltpu.SemaphoreType.DMA(shape)] * 2
    return pl.pallas_call(
        functools.partial(whole_body, nc, nt),
        out_shape=(arr(*sky.shape), arr(*dual.shape)),
        in_specs=[VMEM] * 7 + [SMEM] * 3,
        out_specs=(VMEM, VMEM),
        scratch_shapes=scratch,
        compiler_params=pltpu.CompilerParams(
            vmem_limit_bytes=60 * 1024 * 1024, collective_id=0, has_side_effects=True
        ),
        name="primal_dual",
    )(
        sky,
        dual,
        phase[0, 0],
        rows_at[0, 0][:, None],
        rows_at[0, 0][None, :],
        weight[0, 0],
        vis_data[0, 0],
        filters.reshape(-1),
        level_counts,
        radius,
    )


def solution(mesh):
    placed = (
        P(None, "tblk", "chan"),
        P(None, None, "tblk", "chan"),
        P("chan", "tblk", None, None),
        P("chan", "tblk", None),
        P("chan", "tblk", None, None),
        P("chan", "tblk", None, None, None),
        P(),
        P(),
        P(),
    )
    return jax.shard_map(
        per_device,
        mesh=mesh,
        in_specs=placed,
        out_specs=(P(None, "tblk", "chan"), P(None, None, "tblk", "chan")),
        check_vma=False,
    )
```
